32 devices in a mesh: parts: 1, query: 16 (over z, y, x), blk: 2 (over core).
Axes of the slice: x: 2, y: 2, z: 4, core: 2. Of those that a mesh axis runs over, the one named last changes fastest.
Arguments:
- queries: bfloat16 [2, 256, 16384], P('blk', ('parts', 'query')), may hold values from -600 to 600, as said below
- cameras: bfloat16 [16, 512, 16384], P(('parts', 'query'), 'blk'), may hold values from -600 to 600, as said below
- query_block: int32 [16, 2, 16], P(('parts', 'query'), 'blk'), may hold values from 0 to 1
- camera_block: int32 [16, 2, 16], P(('parts', 'query'), 'blk'), may hold values from 0 to 3
- counts: int32 [16, 2], P(('parts', 'query'), 'blk'), may hold values from 1 to 16, as said below
Outputs:
- scores: float32 [16, 2, 16, 128, 128], P(('parts', 'query'), 'blk')
The draws below stay inside these ranges and needn't reach their ends.
Inputs may be any that keep to these rules, and one draw needn't show every extreme that they name: `queries`: finite values. `cameras`: finite values. `counts`: in every draw some list has all 16 slots live.
All inputs are finite; a program needn't handle non-finite values.
Results may differ from the reference program's by a relative error of at most 0.0003.
Values may be sent and summed in bfloat16 or wider, within the bound.
A program may use at most 192 MiB of HBM per device.

```python
import math
import jax
import jax.numpy as jnp
from jax import lax

F = 16384
BLOCK = 128
KMAX = 16
QROWS = 256
QBLOCKS = 2
CROWS = 512
CBLOCKS = 4
N_QUERY = 16
N_BLK = 2


def scaled_rows(key, shape):
    key_base, key_row, key_col = jax.random.split(key, 3)
    row_shape = (shape[0], shape[1], 1)
    col_shape = (shape[0], 1, shape[2])
    base = jax.random.normal(key_base, shape, jnp.float32)
    upper = math.log(4.0)
    row_scale = jnp.exp(jax.random.uniform(key_row, row_shape, jnp.float32, 0.0, upper))
    col_scale = jnp.exp(jax.random.uniform(key_col, col_shape, jnp.float32, 0.0, upper))
    return jnp.clip(base * row_scale * col_scale, -600.0, 600.0)


def draw_queries(key, part):
    return scaled_rows(jax.random.fold_in(key, 11), (N_BLK, QROWS, F)).astype(jnp.bfloat16)


def draw_cameras(key, part):
    return scaled_rows(jax.random.fold_in(key, 23), (N_QUERY, CROWS, F)).astype(jnp.bfloat16)


def draw_counts(key, part):
    key_load, key_full = jax.random.split(jax.random.fold_in(key, 37))
    loads = jax.random.randint(key_load, (N_QUERY * N_BLK,), 1, KMAX + 1, dtype=jnp.int32)
    spot = jax.random.randint(key_full, (), 0, N_QUERY * N_BLK, dtype=jnp.int32)
    filled = jnp.where(jnp.arange(N_QUERY * N_BLK, dtype=jnp.int32) == spot, KMAX, loads)
    return filled.reshape(N_QUERY, N_BLK).astype(jnp.int32)


def place_ends(result, key, smallest, high):
    extent = result.shape
    spot = [jax.random.randint(jax.random.fold_in(key, axis), (), 0, extent[axis]) for axis in range(len(extent))]
    result = result.at[tuple(spot)].set(smallest)
    longest = extent.index(max(extent))
    spot[longest] = (spot[longest] + 1) % extent[longest]
    return result.at[tuple(spot)].set(high)


def setup_inputs(seed: int = 0, part: int = 0) -> dict:
    streams_of = jax.random.split(jax.random.key(seed), 6)
    own_keys = jax.random.split(jax.random.fold_in(streams_of[5], part), 6)
    queries = draw_queries(jax.random.fold_in(jax.random.fold_in(streams_of[5], part), 71), part)
    cameras = draw_cameras(jax.random.fold_in(jax.random.fold_in(streams_of[5], part), 71), part)
    query_block = place_ends(jax.random.randint(own_keys[2], (N_QUERY, N_BLK, KMAX), 0, QBLOCKS), jax.random.fold_in(own_keys[2], 1), 0, QBLOCKS - 1).astype(jnp.int32)
    camera_block = place_ends(jax.random.randint(own_keys[3], (N_QUERY, N_BLK, KMAX), 0, CBLOCKS), jax.random.fold_in(own_keys[3], 1), 0, CBLOCKS - 1).astype(jnp.int32)
    counts = draw_counts(jax.random.fold_in(jax.random.fold_in(streams_of[5], part), 71), part)
    return dict(queries=queries, cameras=cameras, query_block=query_block, camera_block=camera_block, counts=counts)


def inverse_rms(values):
    wide = values.astype(jnp.float32)
    return lax.rsqrt(lax.optimization_barrier(jnp.mean(wide * wide, axis=-1)) + 1e-06)

def reference(queries, cameras, query_block, camera_block, counts):
    query_scale = inverse_rms(queries)
    camera_scale = inverse_rms(cameras)
    inv_root = 1.0 / math.sqrt(F)
    entries = jnp.arange(N_QUERY * N_BLK * KMAX, dtype=jnp.int32)

    def score_entry(entry_index):
        group_index = entry_index // (N_BLK * KMAX)
        set_index = entry_index // KMAX % N_BLK
        slot_index = entry_index % KMAX
        query_start = (query_block[group_index, set_index, slot_index] * BLOCK).astype(jnp.int32)
        camera_start = (camera_block[group_index, set_index, slot_index] * BLOCK).astype(jnp.int32)
        zero_index = jnp.zeros((), jnp.int32)
        query_rows = lax.dynamic_slice(queries, (set_index, query_start, zero_index), (1, BLOCK, F))[0]
        camera_rows = lax.dynamic_slice(cameras, (group_index, camera_start, zero_index), (1, BLOCK, F))[0]
        products = lax.dot_general(query_rows, camera_rows, (((1,), (1,)), ((), ())), preferred_element_type=jnp.float32)
        query_norms = lax.dynamic_slice(query_scale, (set_index, query_start), (1, BLOCK))[0]
        camera_norms = lax.dynamic_slice(camera_scale, (group_index, camera_start), (1, BLOCK))[0]
        scored = products * query_norms[:, None] * camera_norms[None, :] * inv_root
        return jnp.where(slot_index < counts[group_index, set_index], scored, jnp.zeros_like(scored))
    scores = lax.map(score_entry, entries)
    return scores.reshape(N_QUERY, N_BLK, KMAX, BLOCK, BLOCK)
```

```python
import math

import jax
import jax.numpy as jnp
from jax import lax
from jax.experimental import pallas as pl
from jax.experimental.pallas import tpu as pltpu
from jax.sharding import PartitionSpec as P

BLOCK = 128
CHUNKS = 8
ORDERS = ("zxy", "zyx", "xyz", "zxy", "zyx", "yxz", "zxy", "zyx")
SUB = 512
MESH = pl.DeviceIdType.MESH


def passed_along(x, axis, by):
    devices = lax.axis_size(axis)
    return lax.ppermute(x, axis, [(i, (i + by) % devices) for i in range(devices)])


def inverse_rms(values):
    wide = values.astype(jnp.float32)
    return lax.rsqrt(jnp.mean(wide * wide, axis=-1) + 1e-06)


def line_shards(queries, cameras, query_block, camera_block, counts):
    feature_count = queries.shape[2]
    panel = lax.all_gather(queries[0], "query", axis=0, tiled=True)
    query_scale = inverse_rms(panel)
    tile_rows = cameras.shape[1]
    core_count = lax.axis_size("blk")
    current = cameras[0]
    tile_list = [current]
    for _ in range(core_count - 1):
        current = passed_along(current, "blk", 1)
        tile_list.append(current)
    camera_stack = jnp.concatenate(tile_list, axis=0)
    camera_scale = inverse_rms(camera_stack)
    my_core = lax.axis_index("blk")
    slot_total = query_block.shape[2]
    inv_root = 1.0 / math.sqrt(feature_count)

    def score_slot(slot_index, results):
        query_start = query_block[0, 0, slot_index] * BLOCK
        camera_global = camera_block[0, 0, slot_index] * BLOCK
        turn = (my_core - camera_global // tile_rows) % core_count
        camera_start = turn * tile_rows + camera_global % tile_rows
        query_rows = lax.dynamic_slice_in_dim(panel, query_start, BLOCK, 0)
        camera_rows = lax.dynamic_slice_in_dim(camera_stack, camera_start, BLOCK, 0)
        products = lax.dot_general(
            query_rows, camera_rows, (((1,), (1,)), ((), ())), preferred_element_type=jnp.float32
        )
        query_norms = lax.dynamic_slice_in_dim(query_scale, query_start, BLOCK, 0)
        camera_norms = lax.dynamic_slice_in_dim(camera_scale, camera_start, BLOCK, 0)
        scored = products * query_norms[:, None] * camera_norms[None, :] * inv_root
        return lax.dynamic_update_index_in_dim(results, scored, slot_index, 0)

    results = lax.fori_loop(
        0, counts[0, 0], score_slot, jnp.zeros((slot_total, BLOCK, BLOCK), jnp.float32)
    )
    return results[None, None]


def box_kernel(
    q_ref, cam_ref, table,
    panel, cams, acc, qacc, cacc,
    local_sem, cam_local_sem, cam_send, cam_recv, recv, send_x, send_y, send_up, send_down, send_fwd,
):
    rows, features = q_ref.shape
    cam_rows = cam_ref.shape[0]
    width = features // CHUNKS
    me = lax.axis_index("query")
    core = lax.axis_index("blk")
    z, y, x = me // 4, (me // 2) % 2, me % 2
    mid = ((z + 1) // 2) % 2 == 1
    near = (z + 1 - 2 * (z % 2), 2 - z // 2, 3 - 3 * (z // 2))
    fwd_z = (3 - z, 3 * (z - 1), 3 * (z - 1))

    def index_of(zz, yy, xx):
        return (zz * 2 + yy) * 2 + xx

    x_peer, y_peer = index_of(z, y, 1 - x), index_of(z, 1 - y, x)
    up, down = me + 4, me - 4

    barrier = pltpu.get_barrier_semaphore()
    pl.semaphore_signal(barrier, inc=1, device_id={"query": x_peer}, device_id_type=MESH)
    pl.semaphore_signal(barrier, inc=1, device_id={"query": y_peer}, device_id_type=MESH)
    pl.semaphore_signal(barrier, inc=1, device_id={"blk": 1 - core}, device_id_type=MESH)

    @pl.when(z < 3)
    def _():
        pl.semaphore_signal(barrier, inc=1, device_id={"query": up}, device_id_type=MESH)

    @pl.when(z > 0)
    def _():
        pl.semaphore_signal(barrier, inc=1, device_id={"query": down}, device_id_type=MESH)

    def own_copy(c):
        return pltpu.make_async_copy(
            q_ref.at[:, pl.ds(c * width, width)],
            panel.at[c, pl.ds(me * rows, rows)],
            local_sem.at[c],
        )

    def cam_local(c):
        return pltpu.make_async_copy(
            cam_ref.at[:, pl.ds(c * width, width)],
            cams.at[c, pl.ds(core * cam_rows, cam_rows)],
            cam_local_sem.at[c],
        )

    def cam_remote(c):
        return pltpu.make_async_remote_copy(
            src_ref=cam_ref.at[:, pl.ds(c * width, width)],
            dst_ref=cams.at[c, pl.ds(core * cam_rows, cam_rows)],
            send_sem=cam_send.at[c],
            recv_sem=cam_recv.at[c],
            device_id={"blk": 1 - core},
            device_id_type=MESH,
        )

    for c in range(CHUNKS):
        own_copy(c).start()

    pl.semaphore_wait(barrier, 4 + ((z + 1) // 2) % 2)

    def block_of(c, owner):
        return panel.at[c, pl.ds(pl.multiple_of(owner * rows, rows), rows)]

    def send(c, owner, sem, target, first=False):
        source = q_ref.at[:, pl.ds(c * width, width)] if first else block_of(c, owner)
        pltpu.make_async_remote_copy(
            src_ref=source,
            dst_ref=block_of(c, owner),
            send_sem=sem.at[c],
            recv_sem=recv.at[c, owner],
            device_id={"query": target},
            device_id_type=MESH,
        ).start()

    def forward(c, owner, dims, first=False):
        if "x" in dims:
            send(c, owner, send_x, x_peer, first)
        if "y" in dims:
            send(c, owner, send_y, y_peer, first)
        if "z" in dims:
            @pl.when(z < 3)
            def _():
                send(c, owner, send_up, up, first)

            @pl.when(z > 0)
            def _():
                send(c, owner, send_down, down, first)

    for c in range(CHUNKS):
        forward(c, me, ORDERS[c], True)
        if c == 1:
            for e in range(CHUNKS):
                cam_remote(e).start()
    for c in range(CHUNKS):
        cam_local(c).start()

    acc[...] = jnp.zeros_like(acc)
    qacc[...] = jnp.zeros_like(qacc)
    cacc[...] = jnp.zeros_like(cacc)

    def squares(ref, c, into, height):
        def step(r, carry):
            at = pl.ds(pl.multiple_of(r * 32, 32), 32)
            total = into[at, :]
            for b in range(width // 128):
                v = ref[c, at, b * 128:(b + 1) * 128].astype(jnp.float32)
                total = total + v * v
            into[at, :] = total
            return carry
        lax.fori_loop(0, height // 32, step, 0)

    def multiply(c):
        def step(b, carry):
            at = pl.ds(pl.multiple_of(b * SUB, SUB), SUB)
            acc[...] += lax.dot_general(
                panel[c, :, at], cams[c, :, at], (((1,), (1,)), ((), ())),
                preferred_element_type=jnp.float32,
            )
            return carry
        lax.fori_loop(0, width // SUB, step, 0)

    def arrived(c, owner):
        pltpu.make_async_copy(block_of(c, owner), block_of(c, owner), recv.at[c, owner]).wait()

    def level(c, h):
        order = ORDERS[c]
        for k in (-1, 0, 1, 2):
            for dx in (0, 1):
                for dy in (0, 1):
                    if k + 1 + dx + dy != h:
                        continue
                    zo = z if k < 0 else near[k]
                    owner = index_of(zo, (y + dy) % 2, (x + dx) % 2)
                    moved = {"z": k >= 0, "x": dx == 1, "y": dy == 1}
                    last = max(i for i in range(3) if moved[order[i]])
                    arrived(c, owner)
                    forward(c, owner, order[last + 1:])
                    if order[last] == "z":
                        @pl.when(mid)
                        def _():
                            send(c, owner, send_fwd, index_of(fwd_z[k], y, x))

    for t in range(CHUNKS + 4):
        for h in (5, 4, 3, 2, 1):
            c = t - (h - 1)
            if 0 <= c < CHUNKS:
                level(c, h)
                if h == 5:
                    own_copy(c).wait()
                    multiply(c)
                    squares(panel, c, qacc, panel.shape[1])
        if t < CHUNKS:
            cam_local(t).wait()
            cam_remote(t).wait_recv()
            squares(cams, t, cacc, cams.shape[1])

    inv_root = 1.0 / math.sqrt(features)
    q_scale = lax.rsqrt(jnp.sum(qacc[...], axis=1, keepdims=True) / features + 1e-06)
    c_sum = jnp.sum(jnp.transpose(cacc[...]), axis=0, keepdims=True)
    c_scale = lax.rsqrt(c_sum / features + 1e-06)
    table[...] = acc[...] * q_scale * c_scale * inv_root

    def drain(c, count, sem):
        part = panel.at[c, pl.ds(0, count * rows)]
        pltpu.make_async_copy(part, part, sem.at[c]).wait()

    for c in range(CHUNKS):
        order = ORDERS[c]
        size = {"x": 2, "y": 2, "z": 4}
        through, total = {}, 1
        for d in order:
            through[d] = total
            total *= size[d]
        drain(c, through["x"], send_x)
        drain(c, through["y"], send_y)
        cam_remote(c).wait_send()

        @pl.when(z < 3)
        def _():
            drain(c, through["z"], send_up)

        @pl.when(z > 0)
        def _():
            drain(c, through["z"], send_down)

        @pl.when(mid)
        def _():
            drain(c, 3 * through["z"], send_fwd)


def pick_kernel(query_block, camera_block, counts, table, out_ref):
    def emit(slot, carry):
        query_at = pl.ds(pl.multiple_of(query_block[slot] * BLOCK, BLOCK), BLOCK)
        camera_at = pl.ds(pl.multiple_of(camera_block[slot] * BLOCK, BLOCK), BLOCK)
        tile = table[query_at, camera_at]
        out_ref[slot] = jnp.where(slot < counts[0], tile, jnp.zeros_like(tile))
        return carry

    lax.fori_loop(0, out_ref.shape[0], emit, 0)


def box_shards(queries, cameras, query_block, camera_block, counts):
    rows, features = queries.shape[1:]
    devices = lax.axis_size("query")
    cam_rows = cameras.shape[1]
    slots = query_block.shape[2]
    width = features // CHUNKS
    smem = pl.BlockSpec(memory_space=pltpu.SMEM)
    hbm = pl.BlockSpec(memory_space=pl.ANY)
    dma = pltpu.SemaphoreType.DMA
    table = pl.pallas_call(
        box_kernel,
        out_shape=jax.ShapeDtypeStruct((devices * rows, 2 * cam_rows), jnp.float32),
        in_specs=[hbm, hbm],
        out_specs=pl.BlockSpec(memory_space=pltpu.VMEM),
        scratch_shapes=[
            pltpu.VMEM((CHUNKS, devices * rows, width), jnp.bfloat16),
            pltpu.VMEM((CHUNKS, 2 * cam_rows, width), jnp.bfloat16),
            pltpu.VMEM((devices * rows, 2 * cam_rows), jnp.float32),
            pltpu.VMEM((devices * rows, 128), jnp.float32),
            pltpu.VMEM((2 * cam_rows, 128), jnp.float32),
            dma((CHUNKS,)),
            dma((CHUNKS,)),
            dma((CHUNKS,)),
            dma((CHUNKS,)),
            dma((CHUNKS, devices)),
            dma((CHUNKS,)),
            dma((CHUNKS,)),
            dma((CHUNKS,)),
            dma((CHUNKS,)),
            dma((CHUNKS,)),
        ],
        compiler_params=pltpu.CompilerParams(
            collective_id=0, has_side_effects=True, vmem_limit_bytes=44 * 1024 * 1024
        ),
        cost_estimate=pl.CostEstimate(flops=2 * 256 * 512 * 16384, bytes_accessed=32 << 20, transcendentals=0),
    )(queries[0], cameras[0])
    out = pl.pallas_call(
        pick_kernel,
        out_shape=jax.ShapeDtypeStruct((slots, BLOCK, BLOCK), jnp.float32),
        in_specs=[smem, smem, smem, pl.BlockSpec(memory_space=pltpu.VMEM)],
        out_specs=pl.BlockSpec(memory_space=pltpu.VMEM),
    )(query_block[0, 0], camera_block[0, 0], counts[0], table)
    return out[None, None]


def solution(mesh):
    placed = (
        P("blk", ("parts", "query"), None),
        P(("parts", "query"), "blk", None),
        P(("parts", "query"), "blk", None),
        P(("parts", "query"), "blk", None),
        P(("parts", "query"), "blk"),
    )
    box = mesh.shape["parts"] == 1 and mesh.shape["query"] == 16 and mesh.shape["blk"] == 2
    return jax.shard_map(
        box_shards if box else line_shards,
        mesh=mesh,
        in_specs=placed,
        out_specs=P(("parts", "query"), "blk", None, None, None),
        check_vma=False,
    )
```

```python
import math

import jax
import jax.numpy as jnp
from jax import lax
from jax.experimental import pallas as pl
from jax.experimental.pallas import tpu as pltpu
from jax.sharding import PartitionSpec as P

BLOCK = 128
CHUNKS = 16
ORDERS = ("zxy", "zyx", "xyz", "zxy", "zyx", "yxz", "zxy", "zyx") * 2
SUB = 512
MESH = pl.DeviceIdType.MESH


def passed_along(x, axis, by):
    devices = lax.axis_size(axis)
    return lax.ppermute(x, axis, [(i, (i + by) % devices) for i in range(devices)])


def inverse_rms(values):
    wide = values.astype(jnp.float32)
    return lax.rsqrt(jnp.mean(wide * wide, axis=-1) + 1e-06)


def line_shards(queries, cameras, query_block, camera_block, counts):
    feature_count = queries.shape[2]
    panel = lax.all_gather(queries[0], "query", axis=0, tiled=True)
    query_scale = inverse_rms(panel)
    tile_rows = cameras.shape[1]
    core_count = lax.axis_size("blk")
    current = cameras[0]
    tile_list = [current]
    for _ in range(core_count - 1):
        current = passed_along(current, "blk", 1)
        tile_list.append(current)
    camera_stack = jnp.concatenate(tile_list, axis=0)
    camera_scale = inverse_rms(camera_stack)
    my_core = lax.axis_index("blk")
    slot_total = query_block.shape[2]
    inv_root = 1.0 / math.sqrt(feature_count)

    def score_slot(slot_index, results):
        query_start = query_block[0, 0, slot_index] * BLOCK
        camera_global = camera_block[0, 0, slot_index] * BLOCK
        turn = (my_core - camera_global // tile_rows) % core_count
        camera_start = turn * tile_rows + camera_global % tile_rows
        query_rows = lax.dynamic_slice_in_dim(panel, query_start, BLOCK, 0)
        camera_rows = lax.dynamic_slice_in_dim(camera_stack, camera_start, BLOCK, 0)
        products = lax.dot_general(
            query_rows, camera_rows, (((1,), (1,)), ((), ())), preferred_element_type=jnp.float32
        )
        query_norms = lax.dynamic_slice_in_dim(query_scale, query_start, BLOCK, 0)
        camera_norms = lax.dynamic_slice_in_dim(camera_scale, camera_start, BLOCK, 0)
        scored = products * query_norms[:, None] * camera_norms[None, :] * inv_root
        return lax.dynamic_update_index_in_dim(results, scored, slot_index, 0)

    results = lax.fori_loop(
        0, counts[0, 0], score_slot, jnp.zeros((slot_total, BLOCK, BLOCK), jnp.float32)
    )
    return results[None, None]


def box_kernel(
    q_ref, cam_ref, table,
    panel, cams, acc, qacc, cacc,
    local_sem, cam_local_sem, cam_send, cam_recv, recv, send_x, send_y, send_up, send_down, send_fwd,
):
    rows, features = q_ref.shape
    cam_rows = cam_ref.shape[0]
    width = features // CHUNKS
    me = lax.axis_index("query")
    core = lax.axis_index("blk")
    z, y, x = me // 4, (me // 2) % 2, me % 2
    mid = ((z + 1) // 2) % 2 == 1
    near = (z + 1 - 2 * (z % 2), 2 - z // 2, 3 - 3 * (z // 2))
    fwd_z = (3 - z, 3 * (z - 1), 3 * (z - 1))

    def index_of(zz, yy, xx):
        return (zz * 2 + yy) * 2 + xx

    x_peer, y_peer = index_of(z, y, 1 - x), index_of(z, 1 - y, x)
    up, down = me + 4, me - 4

    barrier = pltpu.get_barrier_semaphore()
    pl.semaphore_signal(barrier, inc=1, device_id={"query": x_peer}, device_id_type=MESH)
    pl.semaphore_signal(barrier, inc=1, device_id={"query": y_peer}, device_id_type=MESH)
    pl.semaphore_signal(barrier, inc=1, device_id={"blk": 1 - core}, device_id_type=MESH)

    @pl.when(z < 3)
    def _():
        pl.semaphore_signal(barrier, inc=1, device_id={"query": up}, device_id_type=MESH)

    @pl.when(z > 0)
    def _():
        pl.semaphore_signal(barrier, inc=1, device_id={"query": down}, device_id_type=MESH)

    def own_copy(c):
        return pltpu.make_async_copy(
            q_ref.at[:, pl.ds(c * width, width)],
            panel.at[c, pl.ds(me * rows, rows)],
            local_sem.at[c],
        )

    def cam_local(c):
        return pltpu.make_async_copy(
            cam_ref.at[:, pl.ds(c * width, width)],
            cams.at[c, pl.ds(core * cam_rows, cam_rows)],
            cam_local_sem.at[c],
        )

    def cam_remote(c):
        return pltpu.make_async_remote_copy(
            src_ref=cam_ref.at[:, pl.ds(c * width, width)],
            dst_ref=cams.at[c, pl.ds(core * cam_rows, cam_rows)],
            send_sem=cam_send.at[c],
            recv_sem=cam_recv.at[c],
            device_id={"blk": 1 - core},
            device_id_type=MESH,
        )

    for c in range(CHUNKS):
        own_copy(c).start()

    pl.semaphore_wait(barrier, 4 + ((z + 1) // 2) % 2)

    def block_of(c, owner):
        return panel.at[c, pl.ds(pl.multiple_of(owner * rows, rows), rows)]

    def send(c, owner, sem, target, first=False):
        source = q_ref.at[:, pl.ds(c * width, width)] if first else block_of(c, owner)
        pltpu.make_async_remote_copy(
            src_ref=source,
            dst_ref=block_of(c, owner),
            send_sem=sem.at[c],
            recv_sem=recv.at[c, owner],
            device_id={"query": target},
            device_id_type=MESH,
        ).start()

    def forward(c, owner, dims, first=False):
        if "x" in dims:
            send(c, owner, send_x, x_peer, first)
        if "y" in dims:
            send(c, owner, send_y, y_peer, first)
        if "z" in dims:
            @pl.when(z < 3)
            def _():
                send(c, owner, send_up, up, first)

            @pl.when(z > 0)
            def _():
                send(c, owner, send_down, down, first)

    for c in range(CHUNKS):
        forward(c, me, ORDERS[c], True)
        if c == 1:
            for e in range(CHUNKS):
                cam_remote(e).start()
    for c in range(CHUNKS):
        cam_local(c).start()

    acc[...] = jnp.zeros_like(acc)
    qacc[...] = jnp.zeros_like(qacc)
    cacc[...] = jnp.zeros_like(cacc)

    def squares(ref, c, into, height):
        def step(r, carry):
            at = pl.ds(pl.multiple_of(r * 32, 32), 32)
            total = into[at, :]
            for b in range(width // 128):
                v = ref[c, at, b * 128:(b + 1) * 128].astype(jnp.float32)
                total = total + v * v
            into[at, :] = total
            return carry
        lax.fori_loop(0, height // 32, step, 0)

    def multiply(c):
        def step(b, carry):
            at = pl.ds(pl.multiple_of(b * SUB, SUB), SUB)
            acc[...] += lax.dot_general(
                panel[c, :, at], cams[c, :, at], (((1,), (1,)), ((), ())),
                preferred_element_type=jnp.float32,
            )
            return carry
        lax.fori_loop(0, width // SUB, step, 0)

    def arrived(c, owner):
        pltpu.make_async_copy(block_of(c, owner), block_of(c, owner), recv.at[c, owner]).wait()

    def level(c, h):
        order = ORDERS[c]
        for k in (-1, 0, 1, 2):
            for dx in (0, 1):
                for dy in (0, 1):
                    if k + 1 + dx + dy != h:
                        continue
                    zo = z if k < 0 else near[k]
                    owner = index_of(zo, (y + dy) % 2, (x + dx) % 2)
                    moved = {"z": k >= 0, "x": dx == 1, "y": dy == 1}
                    last = max(i for i in range(3) if moved[order[i]])
                    arrived(c, owner)
                    forward(c, owner, order[last + 1:])
                    if order[last] == "z":
                        @pl.when(mid)
                        def _():
                            send(c, owner, send_fwd, index_of(fwd_z[k], y, x))

    for t in range(CHUNKS + 4):
        for h in (5, 4, 3, 2, 1):
            c = t - (h - 1)
            if 0 <= c < CHUNKS:
                level(c, h)
                if h == 5:
                    own_copy(c).wait()
                    multiply(c)
                    squares(panel, c, qacc, panel.shape[1])
        if t < CHUNKS:
            cam_local(t).wait()
            cam_remote(t).wait_recv()
            squares(cams, t, cacc, cams.shape[1])

    inv_root = 1.0 / math.sqrt(features)
    q_scale = lax.rsqrt(jnp.sum(qacc[...], axis=1, keepdims=True) / features + 1e-06)
    c_sum = jnp.sum(jnp.transpose(cacc[...]), axis=0, keepdims=True)
    c_scale = lax.rsqrt(c_sum / features + 1e-06)
    table[...] = acc[...] * q_scale * c_scale * inv_root

    def drain(c, count, sem):
        part = panel.at[c, pl.ds(0, count * rows)]
        pltpu.make_async_copy(part, part, sem.at[c]).wait()

    for c in range(CHUNKS):
        order = ORDERS[c]
        size = {"x": 2, "y": 2, "z": 4}
        through, total = {}, 1
        for d in order:
            through[d] = total
            total *= size[d]
        drain(c, through["x"], send_x)
        drain(c, through["y"], send_y)
        cam_remote(c).wait_send()

        @pl.when(z < 3)
        def _():
            drain(c, through["z"], send_up)

        @pl.when(z > 0)
        def _():
            drain(c, through["z"], send_down)

        @pl.when(mid)
        def _():
            drain(c, 3 * through["z"], send_fwd)


def pick_kernel(query_block, camera_block, counts, table, out_ref):
    def emit(slot, carry):
        query_at = pl.ds(pl.multiple_of(query_block[slot] * BLOCK, BLOCK), BLOCK)
        camera_at = pl.ds(pl.multiple_of(camera_block[slot] * BLOCK, BLOCK), BLOCK)
        tile = table[query_at, camera_at]
        out_ref[slot] = jnp.where(slot < counts[0], tile, jnp.zeros_like(tile))
        return carry

    lax.fori_loop(0, out_ref.shape[0], emit, 0)


def box_shards(queries, cameras, query_block, camera_block, counts):
    rows, features = queries.shape[1:]
    devices = lax.axis_size("query")
    cam_rows = cameras.shape[1]
    slots = query_block.shape[2]
    width = features // CHUNKS
    smem = pl.BlockSpec(memory_space=pltpu.SMEM)
    hbm = pl.BlockSpec(memory_space=pltpu.HBM)
    dma = pltpu.SemaphoreType.DMA
    table = pl.pallas_call(
        box_kernel,
        out_shape=jax.ShapeDtypeStruct((devices * rows, 2 * cam_rows), jnp.float32),
        in_specs=[hbm, hbm],
        out_specs=pl.BlockSpec(memory_space=pltpu.VMEM),
        scratch_shapes=[
            pltpu.VMEM((CHUNKS, devices * rows, width), jnp.bfloat16),
            pltpu.VMEM((CHUNKS, 2 * cam_rows, width), jnp.bfloat16),
            pltpu.VMEM((devices * rows, 2 * cam_rows), jnp.float32),
            pltpu.VMEM((devices * rows, 128), jnp.float32),
            pltpu.VMEM((2 * cam_rows, 128), jnp.float32),
            dma((CHUNKS,)),
            dma((CHUNKS,)),
            dma((CHUNKS,)),
            dma((CHUNKS,)),
            dma((CHUNKS, devices)),
            dma((CHUNKS,)),
            dma((CHUNKS,)),
            dma((CHUNKS,)),
            dma((CHUNKS,)),
            dma((CHUNKS,)),
        ],
        compiler_params=pltpu.CompilerParams(
            collective_id=0, has_side_effects=True, vmem_limit_bytes=44 * 1024 * 1024
        ),
        cost_estimate=pl.CostEstimate(flops=2 * 256 * 512 * 16384, bytes_accessed=32 << 20, transcendentals=0),
    )(queries[0], cameras[0])
    out = pl.pallas_call(
        pick_kernel,
        out_shape=jax.ShapeDtypeStruct((slots, BLOCK, BLOCK), jnp.float32),
        in_specs=[smem, smem, smem, pl.BlockSpec(memory_space=pltpu.VMEM)],
        out_specs=pl.BlockSpec(memory_space=pltpu.VMEM),
    )(query_block[0, 0], camera_block[0, 0], counts[0], table)
    return out[None, None]


def solution(mesh):
    placed = (
        P("blk", ("parts", "query"), None),
        P(("parts", "query"), "blk", None),
        P(("parts", "query"), "blk", None),
        P(("parts", "query"), "blk", None),
        P(("parts", "query"), "blk"),
    )
    box = mesh.shape["parts"] == 1 and mesh.shape["query"] == 16 and mesh.shape["blk"] == 2
    return jax.shard_map(
        box_shards if box else line_shards,
        mesh=mesh,
        in_specs=placed,
        out_specs=P(("parts", "query"), "blk", None, None, None),
        check_vma=False,
    )
```

```python
import math

import jax
import jax.numpy as jnp
from jax import lax
from jax.experimental import pallas as pl
from jax.experimental.pallas import tpu as pltpu
from jax.sharding import PartitionSpec as P

BLOCK = 128
CHUNKS = 16
ORDERS = ("zxy", "zyx", "xyz", "zxy", "zyx", "yxz", "zxy", "zyx") * 2
SUB = 512
WAITS = {"z": (0, 1, 2, 4, 6), "x": (0, 2, 4, 5, 6), "y": (0, 2, 4, 5, 6)}
MESH = pl.DeviceIdType.MESH


def passed_along(x, axis, by):
    devices = lax.axis_size(axis)
    return lax.ppermute(x, axis, [(i, (i + by) % devices) for i in range(devices)])


def inverse_rms(values):
    wide = values.astype(jnp.float32)
    return lax.rsqrt(jnp.mean(wide * wide, axis=-1) + 1e-06)


def line_shards(queries, cameras, query_block, camera_block, counts):
    feature_count = queries.shape[2]
    panel = lax.all_gather(queries[0], "query", axis=0, tiled=True)
    query_scale = inverse_rms(panel)
    tile_rows = cameras.shape[1]
    core_count = lax.axis_size("blk")
    current = cameras[0]
    tile_list = [current]
    for _ in range(core_count - 1):
        current = passed_along(current, "blk", 1)
        tile_list.append(current)
    camera_stack = jnp.concatenate(tile_list, axis=0)
    camera_scale = inverse_rms(camera_stack)
    my_core = lax.axis_index("blk")
    slot_total = query_block.shape[2]
    inv_root = 1.0 / math.sqrt(feature_count)

    def score_slot(slot_index, results):
        query_start = query_block[0, 0, slot_index] * BLOCK
        camera_global = camera_block[0, 0, slot_index] * BLOCK
        turn = (my_core - camera_global // tile_rows) % core_count
        camera_start = turn * tile_rows + camera_global % tile_rows
        query_rows = lax.dynamic_slice_in_dim(panel, query_start, BLOCK, 0)
        camera_rows = lax.dynamic_slice_in_dim(camera_stack, camera_start, BLOCK, 0)
        products = lax.dot_general(
            query_rows, camera_rows, (((1,), (1,)), ((), ())), preferred_element_type=jnp.float32
        )
        query_norms = lax.dynamic_slice_in_dim(query_scale, query_start, BLOCK, 0)
        camera_norms = lax.dynamic_slice_in_dim(camera_scale, camera_start, BLOCK, 0)
        scored = products * query_norms[:, None] * camera_norms[None, :] * inv_root
        return lax.dynamic_update_index_in_dim(results, scored, slot_index, 0)

    results = lax.fori_loop(
        0, counts[0, 0], score_slot, jnp.zeros((slot_total, BLOCK, BLOCK), jnp.float32)
    )
    return results[None, None]


def box_kernel(
    q_ref, cam_ref, table,
    panel, cams, acc, qacc, cacc,
    local_sem, cam_local_sem, cam_send, cam_recv, recv, send_x, send_y, send_up, send_down, send_fwd,
):
    rows, features = q_ref.shape
    cam_rows = cam_ref.shape[0]
    width = features // CHUNKS
    me = lax.axis_index("query")
    core = lax.axis_index("blk")
    z, y, x = me // 4, (me // 2) % 2, me % 2
    mid = ((z + 1) // 2) % 2 == 1
    near = (z + 1 - 2 * (z % 2), 2 - z // 2, 3 - 3 * (z // 2))
    fwd_z = (3 - z, 3 * (z - 1), 3 * (z - 1))

    def index_of(zz, yy, xx):
        return (zz * 2 + yy) * 2 + xx

    x_peer, y_peer = index_of(z, y, 1 - x), index_of(z, 1 - y, x)
    up, down = me + 4, me - 4

    barrier = pltpu.get_barrier_semaphore()
    pl.semaphore_signal(barrier, inc=1, device_id={"query": x_peer}, device_id_type=MESH)
    pl.semaphore_signal(barrier, inc=1, device_id={"query": y_peer}, device_id_type=MESH)
    pl.semaphore_signal(barrier, inc=1, device_id={"blk": 1 - core}, device_id_type=MESH)

    @pl.when(z < 3)
    def _():
        pl.semaphore_signal(barrier, inc=1, device_id={"query": up}, device_id_type=MESH)

    @pl.when(z > 0)
    def _():
        pl.semaphore_signal(barrier, inc=1, device_id={"query": down}, device_id_type=MESH)

    def place(c, zz, yy, xx):
        order = ORDERS[c]
        first, second = (yy, xx) if "xy" in order else (xx, yy)
        if order[0] == "z":
            return (first * 2 + second) * 4 + zz
        return (zz * 2 + first) * 2 + second

    def block_of(c, slot, count=1):
        return panel.at[c, pl.ds(pl.multiple_of(slot * rows, rows), count * rows)]

    def send(c, slot, count, sem, message, target, first=False):
        pltpu.make_async_remote_copy(
            src_ref=q_ref.at[:, pl.ds(c * width, width)] if first else block_of(c, slot, count),
            dst_ref=block_of(c, slot, count),
            send_sem=sem.at[c],
            recv_sem=recv.at[c, message],
            device_id={"query": target},
            device_id_type=MESH,
        ).start()

    def send_line(c, slot, count, first=False):
        @pl.when(z < 3)
        def _():
            send(c, slot, count, send_up, z, up, first)

        @pl.when(z > 0)
        def _():
            send(c, slot, count, send_down, z, down, first)

    across = {"x": (send_x, x_peer), "y": (send_y, y_peer)}

    def send_across(c, d, slot, count, message, first=False):
        sem, peer = across[d]
        send(c, slot, count, sem, message, peer, first)

    def own_copy(c):
        return pltpu.make_async_copy(
            q_ref.at[:, pl.ds(c * width, width)],
            block_of(c, place(c, z, y, x)),
            local_sem.at[c],
        )

    def cam_local(c):
        return pltpu.make_async_copy(
            cam_ref.at[:, pl.ds(c * width, width)],
            cams.at[c, pl.ds(core * cam_rows, cam_rows)],
            cam_local_sem.at[c],
        )

    def cam_remote(c):
        return pltpu.make_async_remote_copy(
            src_ref=cam_ref.at[:, pl.ds(c * width, width)],
            dst_ref=cams.at[c, pl.ds(core * cam_rows, cam_rows)],
            send_sem=cam_send.at[c],
            recv_sem=cam_recv.at[c],
            device_id={"blk": 1 - core},
            device_id_type=MESH,
        )

    for c in range(CHUNKS):
        own_copy(c).start()

    pl.semaphore_wait(barrier, 4 + ((z + 1) // 2) % 2)

    for c in range(CHUNKS):
        if ORDERS[c][0] == "z":
            send_line(c, place(c, z, y, x), 1, True)
        else:
            send_across(c, ORDERS[c][0], place(c, z, y, x), 1, 4, True)
        if c == 1:
            for e in range(CHUNKS):
                cam_remote(e).start()
    for c in range(CHUNKS):
        cam_local(c).start()

    acc[...] = jnp.zeros_like(acc)
    qacc[...] = jnp.zeros_like(qacc)
    cacc[...] = jnp.zeros_like(cacc)

    def squares(ref, c, into, height, row_of):
        def step(r, carry):
            at = pl.ds(pl.multiple_of(r * rows, rows), rows)
            src = pl.ds(pl.multiple_of(row_of(r) * rows, rows), rows)
            total = into[at, :]
            for b in range(width // 128):
                v = ref[c, src, b * 128:(b + 1) * 128].astype(jnp.float32)
                total = total + v * v
            into[at, :] = total
            return carry
        lax.fori_loop(0, height // rows, step, 0, unroll=4)

    def multiply(c):
        slots = [place(c, i // 4, (i // 2) % 2, i % 2) for i in range(16)]

        def step(b, carry):
            at = pl.ds(pl.multiple_of(b * SUB, SUB), SUB)
            left = jnp.concatenate([panel[c, s * rows:(s + 1) * rows, at] for s in slots], axis=0)
            acc[...] += lax.dot_general(
                left, cams[c, :, at], (((1,), (1,)), ((), ())),
                preferred_element_type=jnp.float32,
            )
            return carry
        lax.fori_loop(0, width // SUB, step, 0)

    def arrived(c, slot, count, message):
        part = block_of(c, slot, count)
        pltpu.make_async_copy(part, part, recv.at[c, message]).wait()

    def from_line(c, k, slot, count):
        arrived(c, slot, count, near[k])

        @pl.when(mid)
        def _():
            send(c, slot, count, send_fwd, near[k], index_of(fwd_z[k], y, x))

    def event(c, h):
        order = ORDERS[c]
        line_first = order[0] == "z"
        a, b = order.replace("z", "")
        at = {"x": x, "y": y}
        other = {"x": 1 - x, "y": 1 - y}
        if line_first:
            if h < 3:
                from_line(c, h, place(c, near[h], y, x), 1)
                if h == 2:
                    own_copy(c).wait()
                    send_across(c, a, (at[b] * 2 + at[a]) * 4, 4, 4)
            elif h == 3:
                arrived(c, (at[b] * 2 + other[a]) * 4, 4, 4)
                send_across(c, b, at[b] * 8, 8, 5)
            else:
                arrived(c, other[b] * 8, 8, 5)
        elif h == 0:
            own_copy(c).wait()
            arrived(c, (z * 2 + at[b]) * 2 + other[a], 1, 4)
            send_across(c, b, (z * 2 + at[b]) * 2, 2, 5)
        elif h == 1:
            arrived(c, (z * 2 + other[b]) * 2, 2, 5)
            send_line(c, z * 4, 4)
        else:
            from_line(c, h - 2, near[h - 2] * 4, 4)

    for t in range(CHUNKS + WAITS["z"][-1]):
        for h in (4, 3, 2, 1, 0):
            for c in range(CHUNKS):
                if c + WAITS[ORDERS[c][0]][h] == t:
                    event(c, h)
                    if h == 4:
                        multiply(c)
                        squares(panel, c, qacc, panel.shape[1],
                                lambda r: place(c, r // 4, (r // 2) % 2, r % 2))
        if t < CHUNKS:
            cam_local(t).wait()
            cam_remote(t).wait_recv()
            squares(cams, t, cacc, cams.shape[1], lambda r: r)

    inv_root = 1.0 / math.sqrt(features)
    q_scale = lax.rsqrt(jnp.sum(qacc[...], axis=1, keepdims=True) / features + 1e-06)
    c_sum = jnp.sum(jnp.transpose(cacc[...]), axis=0, keepdims=True)
    c_scale = lax.rsqrt(c_sum / features + 1e-06)
    table[...] = acc[...] * q_scale * c_scale * inv_root

    def drain(c, count, sem):
        part = panel.at[c, pl.ds(0, count * rows)]
        pltpu.make_async_copy(part, part, sem.at[c]).wait()

    for c in range(CHUNKS):
        order = ORDERS[c]
        size = {"x": 2, "y": 2, "z": 4}
        through, total = {}, 1
        for d in order:
            through[d] = total
            total *= size[d]
        drain(c, through["x"], send_x)
        drain(c, through["y"], send_y)
        cam_remote(c).wait_send()

        @pl.when(z < 3)
        def _():
            drain(c, through["z"], send_up)

        @pl.when(z > 0)
        def _():
            drain(c, through["z"], send_down)

        @pl.when(mid)
        def _():
            drain(c, 3 * through["z"], send_fwd)


def pick_kernel(query_block, camera_block, counts, table, out_ref):
    def emit(slot, carry):
        query_at = pl.ds(pl.multiple_of(query_block[slot] * BLOCK, BLOCK), BLOCK)
        camera_at = pl.ds(pl.multiple_of(camera_block[slot] * BLOCK, BLOCK), BLOCK)
        tile = table[query_at, camera_at]
        out_ref[slot] = jnp.where(slot < counts[0], tile, jnp.zeros_like(tile))
        return carry

    lax.fori_loop(0, out_ref.shape[0], emit, 0)


def box_shards(queries, cameras, query_block, camera_block, counts):
    rows, features = queries.shape[1:]
    devices = lax.axis_size("query")
    cam_rows = cameras.shape[1]
    slots = query_block.shape[2]
    width = features // CHUNKS
    smem = pl.BlockSpec(memory_space=pltpu.SMEM)
    hbm = pl.BlockSpec(memory_space=pltpu.HBM)
    dma = pltpu.SemaphoreType.DMA
    table = pl.pallas_call(
        box_kernel,
        out_shape=jax.ShapeDtypeStruct((devices * rows, 2 * cam_rows), jnp.float32),
        in_specs=[hbm, hbm],
        out_specs=pl.BlockSpec(memory_space=pltpu.VMEM),
        scratch_shapes=[
            pltpu.VMEM((CHUNKS, devices * rows, width), jnp.bfloat16),
            pltpu.VMEM((CHUNKS, 2 * cam_rows, width), jnp.bfloat16),
            pltpu.VMEM((devices * rows, 2 * cam_rows), jnp.float32),
            pltpu.VMEM((devices * rows, 128), jnp.float32),
            pltpu.VMEM((2 * cam_rows, 128), jnp.float32),
            dma((CHUNKS,)),
            dma((CHUNKS,)),
            dma((CHUNKS,)),
            dma((CHUNKS,)),
            dma((CHUNKS, 6)),
            dma((CHUNKS,)),
            dma((CHUNKS,)),
            dma((CHUNKS,)),
            dma((CHUNKS,)),
            dma((CHUNKS,)),
        ],
        compiler_params=pltpu.CompilerParams(
            collective_id=0, has_side_effects=True, vmem_limit_bytes=60 * 1024 * 1024
        ),
        cost_estimate=pl.CostEstimate(flops=2 * 256 * 512 * 16384, bytes_accessed=32 << 20, transcendentals=0),
    )(queries[0], cameras[0])
    out = pl.pallas_call(
        pick_kernel,
        out_shape=jax.ShapeDtypeStruct((slots, BLOCK, BLOCK), jnp.float32),
        in_specs=[smem, smem, smem, pl.BlockSpec(memory_space=pltpu.VMEM)],
        out_specs=pl.BlockSpec(memory_space=pltpu.VMEM),
    )(query_block[0, 0], camera_block[0, 0], counts[0], table)
    return out[None, None]


def solution(mesh):
    placed = (
        P("blk", ("parts", "query"), None),
        P(("parts", "query"), "blk", None),
        P(("parts", "query"), "blk", None),
        P(("parts", "query"), "blk", None),
        P(("parts", "query"), "blk"),
    )
    box = mesh.shape["parts"] == 1 and mesh.shape["query"] == 16 and mesh.shape["blk"] == 2
    return jax.shard_map(
        box_shards if box else line_shards,
        mesh=mesh,
        in_specs=placed,
        out_specs=P(("parts", "query"), "blk", None, None, None),
        check_vma=False,
    )
```

```python
import math

import jax
import jax.numpy as jnp
from jax import lax
from jax.experimental import pallas as pl
from jax.experimental.pallas import tpu as pltpu
from jax.sharding import PartitionSpec as P

BLOCK = 128
CHUNKS = 16
ORDERS = ("zxy", "zyx", "xyz", "zxy", "zyx", "yxz", "zxy", "zyx") * 2
SUB = 512
WAITS = {"z": (1, 3, 6, 10, 14), "x": (1, 5, 9, 12, 14), "y": (1, 5, 9, 12, 14)}
MESH = pl.DeviceIdType.MESH


def passed_along(x, axis, by):
    devices = lax.axis_size(axis)
    return lax.ppermute(x, axis, [(i, (i + by) % devices) for i in range(devices)])


def inverse_rms(values):
    wide = values.astype(jnp.float32)
    return lax.rsqrt(jnp.mean(wide * wide, axis=-1) + 1e-06)


def line_shards(queries, cameras, query_block, camera_block, counts):
    feature_count = queries.shape[2]
    panel = lax.all_gather(queries[0], "query", axis=0, tiled=True)
    query_scale = inverse_rms(panel)
    tile_rows = cameras.shape[1]
    core_count = lax.axis_size("blk")
    current = cameras[0]
    tile_list = [current]
    for _ in range(core_count - 1):
        current = passed_along(current, "blk", 1)
        tile_list.append(current)
    camera_stack = jnp.concatenate(tile_list, axis=0)
    camera_scale = inverse_rms(camera_stack)
    my_core = lax.axis_index("blk")
    slot_total = query_block.shape[2]
    inv_root = 1.0 / math.sqrt(feature_count)

    def score_slot(slot_index, results):
        query_start = query_block[0, 0, slot_index] * BLOCK
        camera_global = camera_block[0, 0, slot_index] * BLOCK
        turn = (my_core - camera_global // tile_rows) % core_count
        camera_start = turn * tile_rows + camera_global % tile_rows
        query_rows = lax.dynamic_slice_in_dim(panel, query_start, BLOCK, 0)
        camera_rows = lax.dynamic_slice_in_dim(camera_stack, camera_start, BLOCK, 0)
        products = lax.dot_general(
            query_rows, camera_rows, (((1,), (1,)), ((), ())), preferred_element_type=jnp.float32
        )
        query_norms = lax.dynamic_slice_in_dim(query_scale, query_start, BLOCK, 0)
        camera_norms = lax.dynamic_slice_in_dim(camera_scale, camera_start, BLOCK, 0)
        scored = products * query_norms[:, None] * camera_norms[None, :] * inv_root
        return lax.dynamic_update_index_in_dim(results, scored, slot_index, 0)

    results = lax.fori_loop(
        0, counts[0, 0], score_slot, jnp.zeros((slot_total, BLOCK, BLOCK), jnp.float32)
    )
    return results[None, None]


def box_kernel(
    q_ref, cam_ref, table,
    panel, cams, acc, qacc, cacc,
    local_sem, cam_local_sem, cam_send, cam_recv, recv, send_x, send_y, send_up, send_down, send_fwd,
):
    rows, features = q_ref.shape
    cam_rows = cam_ref.shape[0]
    width = features // CHUNKS
    me = lax.axis_index("query")
    core = lax.axis_index("blk")
    z, y, x = me // 4, (me // 2) % 2, me % 2
    mid = ((z + 1) // 2) % 2 == 1
    near = (z + 1 - 2 * (z % 2), 2 - z // 2, 3 - 3 * (z // 2))
    fwd_z = (3 - z, 3 * (z - 1), 3 * (z - 1))

    def index_of(zz, yy, xx):
        return (zz * 2 + yy) * 2 + xx

    x_peer, y_peer = index_of(z, y, 1 - x), index_of(z, 1 - y, x)
    up, down = me + 4, me - 4

    barrier = pltpu.get_barrier_semaphore()
    pl.semaphore_signal(barrier, inc=1, device_id={"query": x_peer}, device_id_type=MESH)
    pl.semaphore_signal(barrier, inc=1, device_id={"query": y_peer}, device_id_type=MESH)
    pl.semaphore_signal(barrier, inc=1, device_id={"blk": 1 - core}, device_id_type=MESH)

    @pl.when(z < 3)
    def _():
        pl.semaphore_signal(barrier, inc=1, device_id={"query": up}, device_id_type=MESH)

    @pl.when(z > 0)
    def _():
        pl.semaphore_signal(barrier, inc=1, device_id={"query": down}, device_id_type=MESH)

    def place(c, zz, yy, xx):
        order = ORDERS[c]
        first, second = (yy, xx) if "xy" in order else (xx, yy)
        if order[0] == "z":
            return (first * 2 + second) * 4 + zz
        return (zz * 2 + first) * 2 + second

    def block_of(c, slot, count=1):
        return panel.at[c, pl.ds(pl.multiple_of(slot * rows, rows), count * rows)]

    def send(c, slot, count, sem, message, target, first=False):
        pltpu.make_async_remote_copy(
            src_ref=q_ref.at[:, pl.ds(c * width, width)] if first else block_of(c, slot, count),
            dst_ref=block_of(c, slot, count),
            send_sem=sem.at[c],
            recv_sem=recv.at[c, message],
            device_id={"query": target},
            device_id_type=MESH,
        ).start()

    def send_line(c, slot, count, first=False):
        @pl.when(z < 3)
        def _():
            send(c, slot, count, send_up, z, up, first)

        @pl.when(z > 0)
        def _():
            send(c, slot, count, send_down, z, down, first)

    across = {"x": (send_x, x_peer), "y": (send_y, y_peer)}

    def send_across(c, d, slot, count, message, first=False):
        sem, peer = across[d]
        send(c, slot, count, sem, message, peer, first)

    def own_copy(c):
        return pltpu.make_async_copy(
            q_ref.at[:, pl.ds(c * width, width)],
            block_of(c, place(c, z, y, x)),
            local_sem.at[c],
        )

    def cam_local(c):
        return pltpu.make_async_copy(
            cam_ref.at[:, pl.ds(c * width, width)],
            cams.at[c, pl.ds(core * cam_rows, cam_rows)],
            cam_local_sem.at[c],
        )

    def cam_remote(c):
        return pltpu.make_async_remote_copy(
            src_ref=cam_ref.at[:, pl.ds(c * width, width)],
            dst_ref=cams.at[c, pl.ds(core * cam_rows, cam_rows)],
            send_sem=cam_send.at[c],
            recv_sem=cam_recv.at[c],
            device_id={"blk": 1 - core},
            device_id_type=MESH,
        )

    for c in range(CHUNKS):
        own_copy(c).start()

    pl.semaphore_wait(barrier, 4 + ((z + 1) // 2) % 2)

    for c in range(CHUNKS):
        if ORDERS[c][0] == "z":
            send_line(c, place(c, z, y, x), 1, True)
        else:
            send_across(c, ORDERS[c][0], place(c, z, y, x), 1, 4, True)
        if c == 1:
            for e in range(CHUNKS):
                cam_remote(e).start()
    for c in range(CHUNKS):
        cam_local(c).start()

    acc[...] = jnp.zeros_like(acc)
    qacc[...] = jnp.zeros_like(qacc)
    cacc[...] = jnp.zeros_like(cacc)

    def squares(ref, c, into, height, row_of):
        def step(r, carry):
            at = pl.ds(pl.multiple_of(r * rows, rows), rows)
            src = pl.ds(pl.multiple_of(row_of(r) * rows, rows), rows)
            total = into[at, :]
            for b in range(width // 128):
                v = ref[c, src, b * 128:(b + 1) * 128].astype(jnp.float32)
                total = total + v * v
            into[at, :] = total
            return carry
        lax.fori_loop(0, height // rows, step, 0, unroll=4)

    def multiply(c):
        slots = [place(c, i // 4, (i // 2) % 2, i % 2) for i in range(16)]

        def step(b, carry):
            at = pl.ds(pl.multiple_of(b * SUB, SUB), SUB)
            left = jnp.concatenate([panel[c, s * rows:(s + 1) * rows, at] for s in slots], axis=0)
            acc[...] += lax.dot_general(
                left, cams[c, :, at], (((1,), (1,)), ((), ())),
                preferred_element_type=jnp.float32,
            )
            return carry
        lax.fori_loop(0, width // SUB, step, 0)

    def arrived(c, slot, count, message):
        part = block_of(c, slot, count)
        pltpu.make_async_copy(part, part, recv.at[c, message]).wait()

    def from_line(c, k, slot, count):
        arrived(c, slot, count, near[k])

        @pl.when(mid)
        def _():
            send(c, slot, count, send_fwd, near[k], index_of(fwd_z[k], y, x))

    def event(c, h):
        order = ORDERS[c]
        line_first = order[0] == "z"
        a, b = order.replace("z", "")
        at = {"x": x, "y": y}
        other = {"x": 1 - x, "y": 1 - y}
        if line_first:
            if h < 3:
                from_line(c, h, place(c, near[h], y, x), 1)
                if h == 2:
                    own_copy(c).wait()
                    send_across(c, a, (at[b] * 2 + at[a]) * 4, 4, 4)
            elif h == 3:
                arrived(c, (at[b] * 2 + other[a]) * 4, 4, 4)
                send_across(c, b, at[b] * 8, 8, 5)
            else:
                arrived(c, other[b] * 8, 8, 5)
        elif h == 0:
            own_copy(c).wait()
            arrived(c, (z * 2 + at[b]) * 2 + other[a], 1, 4)
            send_across(c, b, (z * 2 + at[b]) * 2, 2, 5)
        elif h == 1:
            arrived(c, (z * 2 + other[b]) * 2, 2, 5)
            send_line(c, z * 4, 4)
        else:
            from_line(c, h - 2, near[h - 2] * 4, 4)

    for t in range(CHUNKS + WAITS["z"][-1]):
        for h in (4, 3, 2, 1, 0):
            for c in range(CHUNKS):
                if c + WAITS[ORDERS[c][0]][h] == t:
                    event(c, h)
                    if h == 4:
                        multiply(c)
                        squares(panel, c, qacc, panel.shape[1],
                                lambda r: place(c, r // 4, (r // 2) % 2, r % 2))
        if t < CHUNKS:
            cam_local(t).wait()
            cam_remote(t).wait_recv()
            squares(cams, t, cacc, cams.shape[1], lambda r: r)

    inv_root = 1.0 / math.sqrt(features)
    q_scale = lax.rsqrt(jnp.sum(qacc[...], axis=1, keepdims=True) / features + 1e-06)
    c_sum = jnp.sum(jnp.transpose(cacc[...]), axis=0, keepdims=True)
    c_scale = lax.rsqrt(c_sum / features + 1e-06)
    table[...] = acc[...] * q_scale * c_scale * inv_root

    def drain(c, count, sem):
        part = panel.at[c, pl.ds(0, count * rows)]
        pltpu.make_async_copy(part, part, sem.at[c]).wait()

    for c in range(CHUNKS):
        order = ORDERS[c]
        size = {"x": 2, "y": 2, "z": 4}
        through, total = {}, 1
        for d in order:
            through[d] = total
            total *= size[d]
        drain(c, through["x"], send_x)
        drain(c, through["y"], send_y)
        cam_remote(c).wait_send()

        @pl.when(z < 3)
        def _():
            drain(c, through["z"], send_up)

        @pl.when(z > 0)
        def _():
            drain(c, through["z"], send_down)

        @pl.when(mid)
        def _():
            drain(c, 3 * through["z"], send_fwd)


def pick_kernel(query_block, camera_block, counts, table, out_ref):
    def emit(slot, carry):
        query_at = pl.ds(pl.multiple_of(query_block[slot] * BLOCK, BLOCK), BLOCK)
        camera_at = pl.ds(pl.multiple_of(camera_block[slot] * BLOCK, BLOCK), BLOCK)
        tile = table[query_at, camera_at]
        out_ref[slot] = jnp.where(slot < counts[0], tile, jnp.zeros_like(tile))
        return carry

    lax.fori_loop(0, out_ref.shape[0], emit, 0)


def box_shards(queries, cameras, query_block, camera_block, counts):
    rows, features = queries.shape[1:]
    devices = lax.axis_size("query")
    cam_rows = cameras.shape[1]
    slots = query_block.shape[2]
    width = features // CHUNKS
    smem = pl.BlockSpec(memory_space=pltpu.SMEM)
    hbm = pl.BlockSpec(memory_space=pltpu.HBM)
    dma = pltpu.SemaphoreType.DMA
    table = pl.pallas_call(
        box_kernel,
        out_shape=jax.ShapeDtypeStruct((devices * rows, 2 * cam_rows), jnp.float32),
        in_specs=[hbm, hbm],
        out_specs=pl.BlockSpec(memory_space=pltpu.VMEM),
        scratch_shapes=[
            pltpu.VMEM((CHUNKS, devices * rows, width), jnp.bfloat16),
            pltpu.VMEM((CHUNKS, 2 * cam_rows, width), jnp.bfloat16),
            pltpu.VMEM((devices * rows, 2 * cam_rows), jnp.float32),
            pltpu.VMEM((devices * rows, 128), jnp.float32),
            pltpu.VMEM((2 * cam_rows, 128), jnp.float32),
            dma((CHUNKS,)),
            dma((CHUNKS,)),
            dma((CHUNKS,)),
            dma((CHUNKS,)),
            dma((CHUNKS, 6)),
            dma((CHUNKS,)),
            dma((CHUNKS,)),
            dma((CHUNKS,)),
            dma((CHUNKS,)),
            dma((CHUNKS,)),
        ],
        compiler_params=pltpu.CompilerParams(
            collective_id=0, has_side_effects=True, vmem_limit_bytes=60 * 1024 * 1024
        ),
        cost_estimate=pl.CostEstimate(flops=2 * 256 * 512 * 16384, bytes_accessed=32 << 20, transcendentals=0),
    )(queries[0], cameras[0])
    out = pl.pallas_call(
        pick_kernel,
        out_shape=jax.ShapeDtypeStruct((slots, BLOCK, BLOCK), jnp.float32),
        in_specs=[smem, smem, smem, pl.BlockSpec(memory_space=pltpu.VMEM)],
        out_specs=pl.BlockSpec(memory_space=pltpu.VMEM),
    )(query_block[0, 0], camera_block[0, 0], counts[0], table)
    return out[None, None]


def solution(mesh):
    placed = (
        P("blk", ("parts", "query"), None),
        P(("parts", "query"), "blk", None),
        P(("parts", "query"), "blk", None),
        P(("parts", "query"), "blk", None),
        P(("parts", "query"), "blk"),
    )
    box = mesh.shape["parts"] == 1 and mesh.shape["query"] == 16 and mesh.shape["blk"] == 2
    return jax.shard_map(
        box_shards if box else line_shards,
        mesh=mesh,
        in_specs=placed,
        out_specs=P(("parts", "query"), "blk", None, None, None),
        check_vma=False,
    )
```

```python
import math

import jax
import jax.numpy as jnp
from jax import lax
from jax.experimental import pallas as pl
from jax.experimental.pallas import tpu as pltpu
from jax.sharding import PartitionSpec as P

BLOCK = 128
CHUNKS = 16
ORDERS = ("zxy", "zyx", "xyz", "zxy", "zyx", "yxz", "zxy", "zyx") * 2
SUB = 1024
WAITS = {"z": (1, 3, 6, 10, 14), "x": (1, 5, 9, 12, 14), "y": (1, 5, 9, 12, 14)}
MESH = pl.DeviceIdType.MESH


def passed_along(x, axis, by):
    devices = lax.axis_size(axis)
    return lax.ppermute(x, axis, [(i, (i + by) % devices) for i in range(devices)])


def inverse_rms(values):
    wide = values.astype(jnp.float32)
    return lax.rsqrt(jnp.mean(wide * wide, axis=-1) + 1e-06)


def line_shards(queries, cameras, query_block, camera_block, counts):
    feature_count = queries.shape[2]
    panel = lax.all_gather(queries[0], "query", axis=0, tiled=True)
    query_scale = inverse_rms(panel)
    tile_rows = cameras.shape[1]
    core_count = lax.axis_size("blk")
    current = cameras[0]
    tile_list = [current]
    for _ in range(core_count - 1):
        current = passed_along(current, "blk", 1)
        tile_list.append(current)
    camera_stack = jnp.concatenate(tile_list, axis=0)
    camera_scale = inverse_rms(camera_stack)
    my_core = lax.axis_index("blk")
    slot_total = query_block.shape[2]
    inv_root = 1.0 / math.sqrt(feature_count)

    def score_slot(slot_index, results):
        query_start = query_block[0, 0, slot_index] * BLOCK
        camera_global = camera_block[0, 0, slot_index] * BLOCK
        turn = (my_core - camera_global // tile_rows) % core_count
        camera_start = turn * tile_rows + camera_global % tile_rows
        query_rows = lax.dynamic_slice_in_dim(panel, query_start, BLOCK, 0)
        camera_rows = lax.dynamic_slice_in_dim(camera_stack, camera_start, BLOCK, 0)
        products = lax.dot_general(
            query_rows, camera_rows, (((1,), (1,)), ((), ())), preferred_element_type=jnp.float32
        )
        query_norms = lax.dynamic_slice_in_dim(query_scale, query_start, BLOCK, 0)
        camera_norms = lax.dynamic_slice_in_dim(camera_scale, camera_start, BLOCK, 0)
        scored = products * query_norms[:, None] * camera_norms[None, :] * inv_root
        return lax.dynamic_update_index_in_dim(results, scored, slot_index, 0)

    results = lax.fori_loop(
        0, counts[0, 0], score_slot, jnp.zeros((slot_total, BLOCK, BLOCK), jnp.float32)
    )
    return results[None, None]


def box_kernel(
    q_ref, cam_ref, table,
    panel, cams, acc, qacc, cacc,
    local_sem, cam_local_sem, cam_send, cam_recv, recv, send_x, send_y, send_up, send_down, send_fwd,
):
    rows, features = q_ref.shape
    cam_rows = cam_ref.shape[0]
    width = features // CHUNKS
    me = lax.axis_index("query")
    core = lax.axis_index("blk")
    z, y, x = me // 4, (me // 2) % 2, me % 2
    mid = ((z + 1) // 2) % 2 == 1
    near = (z + 1 - 2 * (z % 2), 2 - z // 2, 3 - 3 * (z // 2))
    fwd_z = (3 - z, 3 * (z - 1), 3 * (z - 1))

    def index_of(zz, yy, xx):
        return (zz * 2 + yy) * 2 + xx

    x_peer, y_peer = index_of(z, y, 1 - x), index_of(z, 1 - y, x)
    up, down = me + 4, me - 4

    barrier = pltpu.get_barrier_semaphore()
    pl.semaphore_signal(barrier, inc=1, device_id={"query": x_peer}, device_id_type=MESH)
    pl.semaphore_signal(barrier, inc=1, device_id={"query": y_peer}, device_id_type=MESH)
    pl.semaphore_signal(barrier, inc=1, device_id={"blk": 1 - core}, device_id_type=MESH)

    @pl.when(z < 3)
    def _():
        pl.semaphore_signal(barrier, inc=1, device_id={"query": up}, device_id_type=MESH)

    @pl.when(z > 0)
    def _():
        pl.semaphore_signal(barrier, inc=1, device_id={"query": down}, device_id_type=MESH)

    def place(c, zz, yy, xx):
        order = ORDERS[c]
        first, second = (yy, xx) if "xy" in order else (xx, yy)
        if order[0] == "z":
            return (first * 2 + second) * 4 + zz
        return (zz * 2 + first) * 2 + second

    def block_of(c, slot, count=1):
        return panel.at[c, pl.ds(pl.multiple_of(slot * rows, rows), count * rows)]

    def send(c, slot, count, sem, message, target, first=False):
        pltpu.make_async_remote_copy(
            src_ref=q_ref.at[:, pl.ds(c * width, width)] if first else block_of(c, slot, count),
            dst_ref=block_of(c, slot, count),
            send_sem=sem.at[c],
            recv_sem=recv.at[c, message],
            device_id={"query": target},
            device_id_type=MESH,
        ).start()

    def send_line(c, slot, count, first=False):
        @pl.when(z < 3)
        def _():
            send(c, slot, count, send_up, z, up, first)

        @pl.when(z > 0)
        def _():
            send(c, slot, count, send_down, z, down, first)

    across = {"x": (send_x, x_peer), "y": (send_y, y_peer)}

    def send_across(c, d, slot, count, message, first=False):
        sem, peer = across[d]
        send(c, slot, count, sem, message, peer, first)

    def own_copy(c):
        return pltpu.make_async_copy(
            q_ref.at[:, pl.ds(c * width, width)],
            block_of(c, place(c, z, y, x)),
            local_sem.at[c],
        )

    def cam_local(c):
        return pltpu.make_async_copy(
            cam_ref.at[:, pl.ds(c * width, width)],
            cams.at[c, pl.ds(core * cam_rows, cam_rows)],
            cam_local_sem.at[c],
        )

    def cam_remote(c):
        return pltpu.make_async_remote_copy(
            src_ref=cam_ref.at[:, pl.ds(c * width, width)],
            dst_ref=cams.at[c, pl.ds(core * cam_rows, cam_rows)],
            send_sem=cam_send.at[c],
            recv_sem=cam_recv.at[c],
            device_id={"blk": 1 - core},
            device_id_type=MESH,
        )

    for c in range(CHUNKS):
        own_copy(c).start()

    pl.semaphore_wait(barrier, 4 + ((z + 1) // 2) % 2)

    for c in range(CHUNKS):
        if ORDERS[c][0] == "z":
            send_line(c, place(c, z, y, x), 1, True)
        else:
            send_across(c, ORDERS[c][0], place(c, z, y, x), 1, 4, True)
        if c == 1:
            for e in range(CHUNKS):
                cam_remote(e).start()
    for c in range(CHUNKS):
        cam_local(c).start()

    acc[...] = jnp.zeros_like(acc)
    qacc[...] = jnp.zeros_like(qacc)
    cacc[...] = jnp.zeros_like(cacc)

    def squares(ref, c, into, height, row_of):
        def step(r, carry):
            at = pl.ds(pl.multiple_of(r * rows, rows), rows)
            src = pl.ds(pl.multiple_of(row_of(r) * rows, rows), rows)
            total = into[at, :]
            for b in range(width // 128):
                v = ref[c, src, b * 128:(b + 1) * 128].astype(jnp.float32)
                total = total + v * v
            into[at, :] = total
            return carry
        lax.fori_loop(0, height // rows, step, 0, unroll=4)

    def multiply(c):
        slots = [place(c, i // 4, (i // 2) % 2, i % 2) for i in range(16)]

        def step(b, carry):
            at = pl.ds(pl.multiple_of(b * SUB, SUB), SUB)
            left = jnp.concatenate([panel[c, s * rows:(s + 1) * rows, at] for s in slots], axis=0)
            acc[...] += lax.dot_general(
                left, cams[c, :, at], (((1,), (1,)), ((), ())),
                preferred_element_type=jnp.float32,
            )
            return carry
        lax.fori_loop(0, width // SUB, step, 0)

    def arrived(c, slot, count, message):
        part = block_of(c, slot, count)
        pltpu.make_async_copy(part, part, recv.at[c, message]).wait()

    def from_line(c, k, slot, count):
        arrived(c, slot, count, near[k])

        @pl.when(mid)
        def _():
            send(c, slot, count, send_fwd, near[k], index_of(fwd_z[k], y, x))

    def event(c, h):
        order = ORDERS[c]
        line_first = order[0] == "z"
        a, b = order.replace("z", "")
        at = {"x": x, "y": y}
        other = {"x": 1 - x, "y": 1 - y}
        if line_first:
            if h < 3:
                from_line(c, h, place(c, near[h], y, x), 1)
                if h == 2:
                    own_copy(c).wait()
                    send_across(c, a, (at[b] * 2 + at[a]) * 4, 4, 4)
            elif h == 3:
                arrived(c, (at[b] * 2 + other[a]) * 4, 4, 4)
                send_across(c, b, at[b] * 8, 8, 5)
            else:
                arrived(c, other[b] * 8, 8, 5)
        elif h == 0:
            own_copy(c).wait()
            arrived(c, (z * 2 + at[b]) * 2 + other[a], 1, 4)
            send_across(c, b, (z * 2 + at[b]) * 2, 2, 5)
        elif h == 1:
            arrived(c, (z * 2 + other[b]) * 2, 2, 5)
            send_line(c, z * 4, 4)
        else:
            from_line(c, h - 2, near[h - 2] * 4, 4)

    for t in range(CHUNKS + WAITS["z"][-1]):
        for h in (4, 3, 2, 1, 0):
            for c in range(CHUNKS):
                if c + WAITS[ORDERS[c][0]][h] == t:
                    event(c, h)
                    if h == 4:
                        multiply(c)
                        squares(panel, c, qacc, panel.shape[1],
                                lambda r: place(c, r // 4, (r // 2) % 2, r % 2))
        if t < CHUNKS:
            cam_local(t).wait()
            cam_remote(t).wait_recv()
            squares(cams, t, cacc, cams.shape[1], lambda r: r)

    inv_root = 1.0 / math.sqrt(features)
    q_scale = lax.rsqrt(jnp.sum(qacc[...], axis=1, keepdims=True) / features + 1e-06)
    c_sum = jnp.sum(jnp.transpose(cacc[...]), axis=0, keepdims=True)
    c_scale = lax.rsqrt(c_sum / features + 1e-06)
    table[...] = acc[...] * q_scale * c_scale * inv_root

    def drain(c, count, sem):
        part = panel.at[c, pl.ds(0, count * rows)]
        pltpu.make_async_copy(part, part, sem.at[c]).wait()

    for c in range(CHUNKS):
        order = ORDERS[c]
        size = {"x": 2, "y": 2, "z": 4}
        through, total = {}, 1
        for d in order:
            through[d] = total
            total *= size[d]
        drain(c, through["x"], send_x)
        drain(c, through["y"], send_y)
        cam_remote(c).wait_send()

        @pl.when(z < 3)
        def _():
            drain(c, through["z"], send_up)

        @pl.when(z > 0)
        def _():
            drain(c, through["z"], send_down)

        @pl.when(mid)
        def _():
            drain(c, 3 * through["z"], send_fwd)


def pick_kernel(query_block, camera_block, counts, table, out_ref):
    def emit(slot, carry):
        query_at = pl.ds(pl.multiple_of(query_block[slot] * BLOCK, BLOCK), BLOCK)
        camera_at = pl.ds(pl.multiple_of(camera_block[slot] * BLOCK, BLOCK), BLOCK)
        tile = table[query_at, camera_at]
        out_ref[slot] = jnp.where(slot < counts[0], tile, jnp.zeros_like(tile))
        return carry

    lax.fori_loop(0, out_ref.shape[0], emit, 0)


def box_shards(queries, cameras, query_block, camera_block, counts):
    rows, features = queries.shape[1:]
    devices = lax.axis_size("query")
    cam_rows = cameras.shape[1]
    slots = query_block.shape[2]
    width = features // CHUNKS
    smem = pl.BlockSpec(memory_space=pltpu.SMEM)
    hbm = pl.BlockSpec(memory_space=pltpu.HBM)
    dma = pltpu.SemaphoreType.DMA
    table = pl.pallas_call(
        box_kernel,
        out_shape=jax.ShapeDtypeStruct((devices * rows, 2 * cam_rows), jnp.float32),
        in_specs=[hbm, hbm],
        out_specs=pl.BlockSpec(memory_space=pltpu.VMEM),
        scratch_shapes=[
            pltpu.VMEM((CHUNKS, devices * rows, width), jnp.bfloat16),
            pltpu.VMEM((CHUNKS, 2 * cam_rows, width), jnp.bfloat16),
            pltpu.VMEM((devices * rows, 2 * cam_rows), jnp.float32),
            pltpu.VMEM((devices * rows, 128), jnp.float32),
            pltpu.VMEM((2 * cam_rows, 128), jnp.float32),
            dma((CHUNKS,)),
            dma((CHUNKS,)),
            dma((CHUNKS,)),
            dma((CHUNKS,)),
            dma((CHUNKS, 6)),
            dma((CHUNKS,)),
            dma((CHUNKS,)),
            dma((CHUNKS,)),
            dma((CHUNKS,)),
            dma((CHUNKS,)),
        ],
        compiler_params=pltpu.CompilerParams(
            collective_id=0, has_side_effects=True, vmem_limit_bytes=60 * 1024 * 1024
        ),
        cost_estimate=pl.CostEstimate(flops=2 * 256 * 512 * 16384, bytes_accessed=32 << 20, transcendentals=0),
    )(queries[0], cameras[0])
    out = pl.pallas_call(
        pick_kernel,
        out_shape=jax.ShapeDtypeStruct((slots, BLOCK, BLOCK), jnp.float32),
        in_specs=[smem, smem, smem, pl.BlockSpec(memory_space=pltpu.VMEM)],
        out_specs=pl.BlockSpec(memory_space=pltpu.VMEM),
    )(query_block[0, 0], camera_block[0, 0], counts[0], table)
    return out[None, None]


def solution(mesh):
    placed = (
        P("blk", ("parts", "query"), None),
        P(("parts", "query"), "blk", None),
        P(("parts", "query"), "blk", None),
        P(("parts", "query"), "blk", None),
        P(("parts", "query"), "blk"),
    )
    box = mesh.shape["parts"] == 1 and mesh.shape["query"] == 16 and mesh.shape["blk"] == 2
    return jax.shard_map(
        box_shards if box else line_shards,
        mesh=mesh,
        in_specs=placed,
        out_specs=P(("parts", "query"), "blk", None, None, None),
        check_vma=False,
    )
```
